32 devices in a mesh: lon: 8 (over z, x), lat: 4 (over y, core).
Axes of the slice: x: 2, y: 2, z: 4, core: 2. Of those that a mesh axis runs over, the one named last changes fastest.
Arguments:
- thermal_departure: float32 [90, 128, 1024], P(None, 'lat', 'lon'), may hold values from -6 to 6
- moisture_profile: float32 [90, 128, 1024], P(None, 'lat', 'lon'), may hold values from -6 to 6
- solar_elevation_factor: float32 [128, 1024], P('lat', 'lon'), may hold values from 0.1 to 1
- daylight_groups: int32 [128, 8], P('lat', 'lon'), may hold values from 0 to 1, as said below
- spreading_factor: float32 [128, 1024], P('lat', 'lon'), may hold values from 0.03 to 0.24
- entry_layer_matrix: float32 [512, 181], replicated, may hold values from -0.4375 to 0.4375
- entry_layer_offset: float32 [512], replicated, may hold values from -3 to 3
- inner_layer_matrices: float32 [2, 512, 512], replicated, may hold values from -0.25 to 0.25
- inner_layer_offsets: float32 [2, 512], replicated, may hold values from -3 to 3
- final_layer_matrix: float32 [90, 512], replicated, may hold values from -0.25 to 0.25
- final_layer_offset: float32 [90], replicated, may hold values from -3 to 3
Outputs:
- heating: float32 [90, 128, 1024], P(None, 'lat', 'lon')
- temp_next: float32 [90, 128, 1024], P(None, 'lat', 'lon')
The draws below stay inside these ranges and needn't reach their ends.
Inputs may be any that keep to these rules, and one draw needn't show every extreme that they name: In every row the sunlit strips form one run of 4 consecutive strips, wrapping around, so daylight_groups[r, j] + daylight_groups[r, (j + 4) mod 8] == 1; row r and row r + 32 are complements of each other.
All inputs are finite; a program needn't handle non-finite values.
Results may differ from the reference program's by a relative error of at most 0.0001.
Values sent between devices are 32-bit elements; how exact they have to be, the bound alone decides.
A program may use at most 64 MiB of HBM per device.

```python
import math
import jax
import jax.numpy as jnp
from jax import lax

ALTITUDE_TIERS = 90
HID = 512
DEPTH = 2
BLOCK = 128
NB = 32
STEPS = 2
FEAT = 181
MERIDIAN_SPAN = 128
ZONAL_SPAN = 1024
STRIPS = 8


def draw_daylight_groups(key, part):
    key_base = jax.random.fold_in(key, 11)
    key_jitter = jax.random.fold_in(key, 23)
    base = jax.random.randint(key_base, (), 0, STRIPS)
    jitter_local = jax.random.randint(key_jitter, (NB,), -1, 2)
    row_index = jnp.arange(MERIDIAN_SPAN, dtype=jnp.int32)
    band_flip = jnp.mod(row_index // NB, 2) * (STRIPS // 2)
    jitter = jitter_local[jnp.mod(row_index, NB)] + band_flip
    strip = jnp.arange(STRIPS, dtype=jnp.int32)
    offset = jnp.mod(strip[None, :] - base - jitter[:, None], STRIPS)
    return jnp.where(offset < STRIPS // 2, 1, 0).astype(jnp.int32)


def block_scale(key, extent, pieces, low, top_value):
    loudness = 1.0
    for position, blocks in pieces:
        steps = jax.random.uniform(jax.random.fold_in(jax.random.fold_in(key, 6), position), (blocks,), jnp.float32, low / len(pieces), top_value / len(pieces))
        loudness = loudness * jnp.repeat(jnp.exp(steps), extent[position] // blocks).reshape((-1,) + (1,) * (len(extent) - 1 - position))
    return loudness


def bell_draw(own_key, shape, spread, reach, split=(), held_as=jnp.bfloat16):
    values = spread * jax.random.normal(own_key, shape, jnp.float32)
    if split:
        values = values * block_scale(own_key, shape, split, -0.22, 0.18)
    return jnp.clip(values, -reach, reach).astype(held_as)


def setup_inputs(seed: int = 0) -> dict:
    seeds = jax.random.split(jax.random.key(seed), 12)
    return {
        "thermal_departure": bell_draw(seeds[0], (ALTITUDE_TIERS, MERIDIAN_SPAN, ZONAL_SPAN), 1.0, 6.0, ((1, 4), (2, 8)), jnp.float32),
        "moisture_profile": bell_draw(seeds[1], (ALTITUDE_TIERS, MERIDIAN_SPAN, ZONAL_SPAN), 1.0, 6.0, ((1, 4), (2, 8)), jnp.float32),
        "solar_elevation_factor": jnp.clip(0.1 + 0.9 * jax.random.uniform(seeds[2], (MERIDIAN_SPAN, ZONAL_SPAN), jnp.float32) ** block_scale(seeds[2], (MERIDIAN_SPAN, ZONAL_SPAN), ((0, 4), (1, 8)), -0.2, 0.2), 0.1, 1.0),
        "daylight_groups": draw_daylight_groups(jax.random.fold_in(seeds[11], 71), 0),
        "spreading_factor": jnp.clip(jnp.exp(math.log(0.24) - 2.0794415 * jax.random.uniform(seeds[4], (MERIDIAN_SPAN, ZONAL_SPAN), jnp.float32) ** block_scale(seeds[4], (MERIDIAN_SPAN, ZONAL_SPAN), ((0, 4), (1, 8)), -0.2, 0.2)), 0.03, 0.24),
        "entry_layer_matrix": bell_draw(seeds[5], (HID, FEAT), FEAT ** -0.5, 0.4375, (), jnp.float32),
        "entry_layer_offset": bell_draw(seeds[6], (HID,), 0.5, 3.0, (), jnp.float32),
        "inner_layer_matrices": bell_draw(seeds[7], (DEPTH, HID, HID), HID ** -0.5, 0.25, (), jnp.float32),
        "inner_layer_offsets": bell_draw(seeds[8], (DEPTH, HID), 0.5, 3.0, (), jnp.float32),
        "final_layer_matrix": bell_draw(seeds[9], (ALTITUDE_TIERS, HID), HID ** -0.5, 0.25, (), jnp.float32),
        "final_layer_offset": bell_draw(seeds[10], (ALTITUDE_TIERS,), 0.5, 3.0, (), jnp.float32),
    }


def network_apply(columns, entry_layer_matrix, entry_layer_offset, inner_layer_matrices, inner_layer_offsets, final_layer_matrix, final_layer_offset):
    hidden = jax.nn.silu(jnp.dot(entry_layer_matrix, columns, precision=lax.Precision.HIGHEST) + entry_layer_offset[:, None])
    for layer in range(DEPTH):
        hidden = jax.nn.silu(jnp.dot(inner_layer_matrices[layer], hidden, precision=lax.Precision.HIGHEST) + inner_layer_offsets[layer][:, None])
    return jnp.dot(final_layer_matrix, hidden, precision=lax.Precision.HIGHEST) + final_layer_offset[:, None]


def diffuse(atmosphere_snapshot, spreading_factor):
    padded = jnp.concatenate([atmosphere_snapshot[:, :, -1:], atmosphere_snapshot, atmosphere_snapshot[:, :, :1]], axis=2)
    padded = jnp.pad(padded, ((0, 0), (1, 1), (0, 0)))
    beside_all = padded[:, :-2, 1:-1] + padded[:, 2:, 1:-1] + padded[:, 1:-1, :-2] + padded[:, 1:-1, 2:]
    return atmosphere_snapshot + spreading_factor[None] * (beside_all - 4.0 * atmosphere_snapshot)


def reference(thermal_departure, moisture_profile, solar_elevation_factor, daylight_groups, spreading_factor, entry_layer_matrix, entry_layer_offset, inner_layer_matrices, inner_layer_offsets, final_layer_matrix, final_layer_offset):
    thermal_tracks = jnp.moveaxis(thermal_departure, 1, 0)
    moisture_tracks = jnp.moveaxis(moisture_profile, 1, 0)

    def single_parallel(packed):
        temp_row, humid_row, cos_row, lit_row = packed
        columns = jnp.concatenate([temp_row, humid_row, cos_row[None]], axis=0)
        output = network_apply(columns, entry_layer_matrix, entry_layer_offset, inner_layer_matrices, inner_layer_offsets, final_layer_matrix, final_layer_offset)
        lit_cols = jnp.repeat(lit_row.astype(jnp.float32), BLOCK)
        return output * (cos_row * lit_cols)[None]

    warming_tracks = lax.map(single_parallel, (thermal_tracks, moisture_tracks, solar_elevation_factor, daylight_groups))
    heating = jnp.moveaxis(warming_tracks, 0, 1)
    atmosphere_snapshot = thermal_departure
    for substep in range(STEPS):
        atmosphere_snapshot = diffuse(atmosphere_snapshot, spreading_factor)
    return heating, atmosphere_snapshot + heating
```

```python
import jax
import jax.numpy as jnp
from jax import lax
from jax.experimental import pallas as pl
from jax.experimental.pallas import tpu as pltpu
from jax.sharding import PartitionSpec as P

MESH = pl.DeviceIdType.MESH
GROUP = 4
EDGE = 4
PAD = 8
REACH = 2
TAIL = 18


def up(n, m):
    return (n + m - 1) // m * m


def split(x):
    hi = x.astype(jnp.bfloat16)
    lo = (x - hi.astype(jnp.float32)).astype(jnp.bfloat16)
    return hi, lo


def dot(a, b):
    return jnp.dot(a, b, preferred_element_type=jnp.float32)


def gate(h):
    return h + h * jnp.tanh(h)


def tall3(x):
    hi, lo = split(x)
    return jnp.concatenate([hi, lo, hi], axis=0)


def wide3(w):
    hi, lo = split(w)
    return jnp.concatenate([hi, hi, lo], axis=1)


def roll(x, shift, axis):
    return pltpu.roll(x, shift % x.shape[axis], axis)


def kernel(
    temp, moist, mu, lit_h, spread, w0t_h, b0_h, wm_h, bm_h, wf_h, bf_h,
    heat, nxt,
    lit, w0t, b0, wm, bm, wf, bf,
    temp_v, spread_v, own_x, far_x,
    w0_p, w0_c, wm_c, wf_c, b0_c, bm_c, bf_c,
    res_own, res_far,
    temp_t, temp_b, spread_t, spread_b,
    pack, left_m, left_t, left_b, right_m, right_t, right_b,
    edge_0, edge_1, f_all,
    in_sem, own_sem, send_sem, recv_sem, put_sem, out_send, out_recv, halo_send, halo_recv,
    pair_sem,
):
    levels, rows, lanes = temp.shape
    half = rows // 2
    hid = wm_h.shape[1]
    depth = wm_h.shape[0]
    groups = half // GROUP
    feat = w0t_h.shape[0]
    kp = w0_c.shape[1] // 3
    tiles = pack.shape[0] - 1
    slots = lanes // EDGE
    n_lat = lax.axis_size("lat")
    n_lon = lax.axis_size("lon")
    lat = lax.axis_index("lat")
    lon = lax.axis_index("lon")
    parity = lax.rem(lat, 2)
    partner = lat + 1 - 2 * parity
    mine = parity * half
    theirs = half - parity * half
    left = lax.rem(lon + n_lon - 1, n_lon)
    right = lax.rem(lon + 1, n_lon)
    has_up = lat > 0
    has_down = lat < n_lat - 1
    above = jnp.maximum(lat - 1, 0)
    below = jnp.minimum(lat + 1, n_lat - 1)
    leads = parity == 1
    pair_up = lat > 1
    pair_down = lat < n_lat - 2

    def at(lat_to, lon_to):
        return {"lat": lat_to, "lon": lon_to}

    def local(i, src, dst):
        return pltpu.make_async_copy(src, dst, in_sem.at[i])

    small = [
        local(0, lit_h, lit), local(1, w0t_h, w0t), local(2, b0_h, b0),
        local(3, bm_h, bm), local(4, bf_h, bf), local(5, spread, spread_v)]
    large = [local(6, wm_h, wm), local(7, wf_h, wf), local(8, temp, temp_v)]

    def own_start(g):
        for i in range(g * GROUP, (g + 1) * GROUP):
            sem = own_sem.at[g]
            r = mine + i
            pltpu.make_async_copy(temp.at[:, r, :], own_x.at[i, pl.ds(0, levels), :], sem).start()
            pltpu.make_async_copy(moist.at[:, r, :], own_x.at[i, pl.ds(levels, levels), :], sem).start()
            pltpu.make_async_copy(
                mu.at[pl.ds(r, 1), :], own_x.at[i, pl.ds(2 * levels, 1), :], sem).start()

    def group_of(ref, g, count):
        return ref.at[pl.ds(g * GROUP, GROUP), pl.ds(0, count), :]

    def own_wait(g):
        block = group_of(own_x, g, feat)
        pltpu.make_async_copy(block, block, own_sem.at[g]).wait()

    def swap(g, src, dst):
        return pltpu.make_async_remote_copy(
            src_ref=src, dst_ref=dst, send_sem=send_sem.at[g], recv_sem=recv_sem.at[g],
            device_id=at(partner, lon), device_id_type=MESH)

    def far_start(g):
        for i in range(g * GROUP, (g + 1) * GROUP):
            r = theirs + i
            swap(g, temp.at[:, r, :], far_x.at[i, pl.ds(0, levels), :]).start()
            swap(g, moist.at[:, r, :], far_x.at[i, pl.ds(levels, levels), :]).start()
            swap(g, mu.at[pl.ds(r, 1), :], far_x.at[i, pl.ds(2 * levels, 1), :]).start()

    def far_wait(g):
        block = group_of(far_x, g, feat)
        swap(g, block, block).wait()

    barrier = pltpu.get_barrier_semaphore()

    for copy in small:
        copy.start()

    @pl.when(leads)
    def _():
        pl.semaphore_signal(barrier, inc=1, device_id=at(partner, lon), device_id_type=MESH)

    own_start(0)
    own_start(1)

    @pl.when(jnp.logical_not(leads))
    def _():
        pl.semaphore_wait(barrier, 1)
        pl.semaphore_signal(pair_sem, inc=1, device_id=at(partner, lon), device_id_type=MESH)

    @pl.when(leads)
    def _():
        pl.semaphore_wait(pair_sem, 1)

        def hello(lat_to, lon_to):
            pl.semaphore_signal(
                barrier, inc=1, device_id=at(lat_to, lon_to), device_id_type=MESH)

        hello(lat, left)
        hello(lat, right)

        @pl.when(pair_up)
        def _():
            for to in (left, lon, right):
                hello(jnp.maximum(lat - 2, 0), to)

        @pl.when(pair_down)
        def _():
            for to in (left, lon, right):
                hello(jnp.minimum(lat + 2, n_lat - 1), to)

    far_start(0)
    far_start(1)
    large[0].start()
    large[1].start()
    large[2].start()
    for g in range(2, groups):
        far_start(g)
        own_start(g)

    first, last = pl.ds(0, PAD), pl.ds(rows - PAD, PAD)

    def halo(i, src, dst, lat_to, lon_to):
        return pltpu.make_async_remote_copy(
            src_ref=src, dst_ref=dst, send_sem=halo_send.at[i], recv_sem=halo_recv.at[i],
            device_id=at(lat_to, lon_to), device_id_type=MESH)

    beside = [
        halo(0, pack, right_m, lat, left),
        halo(1, pack, left_m, lat, right),
    ]
    to_up = [
        halo(2, spread.at[first, :], spread_b, above, lon),
        halo(3, temp.at[:, pl.ds(0, REACH), :], temp_b.at[:, pl.ds(0, REACH), :], above, lon),
        halo(4, pack.at[:, first, :], right_b, above, left),
        halo(5, pack.at[:, first, :], left_b, above, right),
    ]
    to_down = [
        halo(6, spread.at[last, :], spread_t, below, lon),
        halo(7, temp.at[:, pl.ds(rows - REACH, REACH), :],
             temp_t.at[:, pl.ds(PAD - REACH, REACH), :], below, lon),
        halo(8, pack.at[:, last, :], right_t, below, left),
        halo(9, pack.at[:, last, :], left_t, below, right),
    ]

    def clear(ref):
        ref[...] = jnp.zeros_like(ref)

    w0_p[feat:kp, :] = jnp.zeros((kp - feat, hid), jnp.float32)
    pad = own_x.shape[1] - feat
    for ref in (own_x, far_x):
        ref[:, feat:feat + pad, :] = jnp.zeros((half, pad, lanes), jnp.float32)

    @pl.when(jnp.logical_not(has_up))
    def _():
        for ref in (temp_t, spread_t, left_t, right_t):
            clear(ref)

    @pl.when(jnp.logical_not(has_down))
    def _():
        for ref in (temp_b, spread_b, left_b, right_b):
            clear(ref)

    for copy in small:
        copy.wait()

    def column(row):
        return jnp.broadcast_to(row, (lanes, row.shape[1])).T

    w0_p[0:feat, :] = w0t[...] * 0.5
    w0_c[...] = wide3(w0_p[...].T)
    b0_c[...] = column(b0[...] * 0.5)
    for k in range(depth):
        bm_c[k] = column(bm[k:k + 1, :] * 0.5)
    bf_c[...] = column(bf[...])
    large[0].wait()
    for k in range(depth):
        wm_c[k] = wide3(wm[k] * 0.5)
    large[1].wait()
    wf_c[...] = wide3(wf[...])

    large[2].wait()
    lane = lax.broadcasted_iota(jnp.int32, (rows, lanes), 1)
    for t in range(tiles):
        count = min(slots, levels - t * slots)
        acc = jnp.zeros((rows, lanes), jnp.float32)
        for m in range(count):
            moved = roll(temp_v[t * slots + m], EDGE * m + 2, 1)
            acc = jnp.where(lane // EDGE == m, moved, acc)
        pack[t] = acc
    acc = jnp.where(lane < EDGE, roll(spread_v[...], 2, 1), 0.0)
    step = EDGE
    while step < lanes:
        acc = acc + roll(acc, step, 1)
        step *= 2
    pack[tiles] = acc

    def wide(c):
        return jnp.concatenate([c] * GROUP, axis=1)

    def load(g):
        parts, suns = [], []
        for i in range(g * GROUP, (g + 1) * GROUP):
            on = lit[mine + i].astype(jnp.float32)
            x = own_x[i] * on + far_x[i] * (1.0 - on)
            parts.append(x)
            suns.append(x[2 * levels:2 * levels + 1, :])
        x = jnp.concatenate(parts, axis=1)
        tail = jnp.zeros((kp - x.shape[0], x.shape[1]), jnp.float32)
        return tall3(jnp.concatenate([x, tail], axis=0)), jnp.concatenate(suns, axis=1)

    def put(g, i):
        return pltpu.make_async_copy(
            res_own.at[i], heat.at[:, mine + i, :], put_sem.at[g])

    def send(g, i):
        return pltpu.make_async_remote_copy(
            src_ref=res_far.at[i], dst_ref=heat.at[:, mine + i, :],
            send_sem=out_send.at[g], recv_sem=out_recv.at[g],
            device_id=at(partner, lon), device_id_type=MESH)

    def finish(g, y, sun):
        y = (y + wide(bf_c[...])) * sun
        for j in range(GROUP):
            i = g * GROUP + j
            on = lit[mine + i].astype(jnp.float32)
            value = y[:, j * lanes:(j + 1) * lanes]
            res_far[i] = value * (1.0 - on)
            res_own[i] = value * on
            send(g, i).start()
            put(g, i).start()

    def activate(h, b):
        return tall3(gate(h + wide(b)))

    def pair(g, beside_it):
        a, sun_a = load(g)
        b, sun_b = load(g + 1)
        ya = dot(w0_c[...], a)
        yb = dot(w0_c[...], b)
        a = activate(ya, b0_c[...])
        beside_it(0)
        part = 1
        for k in range(depth):
            ya = dot(wm_c[k], a)
            b = activate(yb, b0_c[...] if k == 0 else bm_c[k - 1])
            beside_it(part)
            yb = dot(wm_c[k], b)
            a = activate(ya, bm_c[k])
            beside_it(part + 1)
            part += 2
        ya = dot(wf_c[...], a)
        b = activate(yb, bm_c[depth - 1])
        beside_it(part)
        finish(g, ya, sun_a)
        yb = dot(wf_c[...], b)
        finish(g + 1, yb, sun_b)

    def greet():
        @pl.when(leads)
        def _():
            pl.semaphore_wait(
                barrier, 2 + 3 * pair_up.astype(jnp.int32) + 3 * pair_down.astype(jnp.int32))
            pl.semaphore_signal(pair_sem, inc=1, device_id=at(partner, lon), device_id_type=MESH)

        @pl.when(jnp.logical_not(leads))
        def _():
            pl.semaphore_wait(pair_sem, 1)

        for copy in beside:
            copy.start()

        @pl.when(has_up)
        def _():
            for copy in to_up:
                copy.start()

        @pl.when(has_down)
        def _():
            for copy in to_down:
                copy.start()

    def early(part):
        if part == 2:
            greet()

    for g in range(2):
        own_wait(g)
        far_wait(g)
    pair(0, early)

    for copy in beside:
        copy.wait()

    @pl.when(has_up)
    def _():
        for copy in to_up:
            copy.wait_send()
        for copy in to_down:
            copy.wait_recv()

    @pl.when(has_down)
    def _():
        for copy in to_down:
            copy.wait_send()
        for copy in to_up:
            copy.wait_recv()

    tall = rows + 2 * PAD

    def stack(top, middle, bottom):
        return jnp.concatenate([top, middle, bottom], axis=0)

    def advance(x, f, west, east):
        around = roll(x, 1, 0) + roll(x, x.shape[0] - 1, 0) + west + east
        return x + f * (around - 4.0 * x)

    slot = lax.broadcasted_iota(jnp.int32, (tall, lanes), 1)
    where = lax.rem(slot, EDGE)
    zero8 = jnp.zeros((PAD, lanes), jnp.float32)

    def gather(t):
        lhs = stack(left_t[t], left_m[t], left_b[t])
        rhs = stack(right_t[t], right_m[t], right_b[t])
        here = stack(zero8, pack[t], zero8)
        return (jnp.where(where < 2, lhs, here), jnp.where(where < 2, here, rhs))

    f_west, f_east = gather(tiles)
    for t in range(tiles):
        west, east = gather(t)
        edge_0[t] = jnp.where(where == 1, roll(east, lanes - 1, 1), roll(west, 1, 1))
        west = advance(west, f_west, roll(west, 1, 1), roll(west, lanes - 1, 1))
        east = advance(east, f_east, roll(east, 1, 1), roll(east, lanes - 1, 1))
        edge_1[t] = jnp.where(where == 1, roll(east, lanes - 1, 1), roll(west, 1, 1))

    f_all[...] = stack(spread_t[...], spread_v[...], spread_b[...])

    def diffuse(k):
        t, m = k // slots, k % slots
        turn = lanes - 2 - EDGE * m
        x = stack(temp_t[k], temp_v[k], temp_b[k])
        rim = roll(edge_0[t], turn, 1)
        west = jnp.where(slot == 0, rim, roll(x, 1, 1))
        east = jnp.where(slot == lanes - 1, rim, roll(x, lanes - 1, 1))
        x = advance(x, f_all[...], west, east)
        core = x[PAD:PAD + rows]
        rim = roll(edge_1[t, PAD:PAD + rows], turn, 1)
        spot = slot[PAD:PAD + rows]
        west = jnp.where(spot == 0, rim, roll(core, 1, 1))
        east = jnp.where(spot == lanes - 1, rim, roll(core, lanes - 1, 1))
        north, south = roll(x, 1, 0)[PAD:PAD + rows], roll(x, tall - 1, 0)[PAD:PAD + rows]
        around = north + south + west + east
        nxt[k] = core + spread_v[...] * (around - 4.0 * core)

    def some(begin, end):
        for k in range(begin, end):
            diffuse(k)

    spread_over = 2 * depth + 2
    bulk = levels - min(TAIL, levels)

    def late(part):
        some(bulk * part // spread_over, bulk * (part + 1) // spread_over)

    for g in range(2, groups, 2):
        own_wait(g)
        own_wait(g + 1)
        far_wait(g)
        far_wait(g + 1)
        pair(g, late if g + 2 == groups else lambda part: None)
    some(bulk, levels)

    for g in range(groups):
        mine_g = res_far.at[pl.ds(g * GROUP, GROUP)]
        pltpu.make_async_remote_copy(
            src_ref=mine_g, dst_ref=mine_g, send_sem=out_send.at[g], recv_sem=out_recv.at[g],
            device_id=at(partner, lon), device_id_type=MESH).wait()
        pltpu.make_async_copy(mine_g, mine_g, put_sem.at[g]).wait()


PARTS = 3


def finish_kernel(heat, nxt, out_heat, out_temp, total, sem):
    levels = heat.shape[0]
    copies = []
    cuts = [levels * p // PARTS for p in range(PARTS + 1)]
    for p in range(PARTS):
        part = pl.ds(cuts[p], cuts[p + 1] - cuts[p])
        copies.append(pltpu.make_async_copy(heat.at[part], out_heat.at[part], sem.at[p]))
        copies[-1].start()
    for p in range(PARTS):
        part = pl.ds(cuts[p], cuts[p + 1] - cuts[p])
        total[part] = nxt[part] + heat[part]
        copies.append(pltpu.make_async_copy(total.at[part], out_temp.at[part], sem.at[PARTS + p]))
        copies[-1].start()
    for copy in copies:
        copy.wait()


def run(temp, moist, mu, lit, spread, w0, b0, wm, bm, wf, bf):
    levels, rows, lanes = temp.shape
    half = rows // 2
    hid = wm.shape[1]
    depth = wm.shape[0]
    feat = w0.shape[1]
    kp = up(feat, 256)
    tall = rows + 2 * PAD
    tiles = (levels * EDGE + lanes - 1) // lanes
    f32, bf16 = jnp.float32, jnp.bfloat16
    vmem = pl.BlockSpec(memory_space=pltpu.VMEM)
    hbm = pl.BlockSpec(memory_space=pltpu.HBM)
    groups = half // GROUP
    dma = pltpu.SemaphoreType.DMA

    def buf(*shape, dtype=f32):
        return pltpu.VMEM(shape, dtype)

    shape = jax.ShapeDtypeStruct(temp.shape, f32)
    heat, nxt = pl.pallas_call(
        kernel,
        out_shape=(shape, shape),
        in_specs=[hbm] * 11,
        out_specs=(vmem, vmem),
        scratch_shapes=[
            pltpu.SMEM((rows,), jnp.int32), buf(feat, hid), buf(1, hid), buf(*wm.shape),
            buf(*bm.shape), buf(*wf.shape), buf(1, levels),
            buf(levels, rows, lanes), buf(rows, lanes),
            buf(half, up(feat, 8), lanes), buf(half, up(feat, 8), lanes),
            buf(kp, hid), buf(hid, 3 * kp, dtype=bf16), buf(depth, hid, 3 * hid, dtype=bf16),
            buf(levels, 3 * hid, dtype=bf16),
            buf(hid, lanes), buf(depth, hid, lanes), buf(levels, lanes),
            buf(half, levels, lanes), buf(half, levels, lanes),
            buf(levels, PAD, lanes), buf(levels, PAD, lanes), buf(PAD, lanes), buf(PAD, lanes),
            buf(tiles + 1, rows, lanes),
            buf(tiles + 1, rows, lanes), buf(tiles + 1, PAD, lanes), buf(tiles + 1, PAD, lanes),
            buf(tiles + 1, rows, lanes), buf(tiles + 1, PAD, lanes), buf(tiles + 1, PAD, lanes),
            buf(tiles, tall, lanes), buf(tiles, tall, lanes), buf(tall, lanes),
            dma((9,)), dma((groups,)), dma((groups,)), dma((groups,)), dma((groups,)),
            dma((groups,)), dma((groups,)), dma((10,)), dma((10,)),
            pltpu.SemaphoreType.REGULAR,
        ],
        compiler_params=pltpu.CompilerParams(
            collective_id=0, has_side_effects=True, vmem_limit_bytes=48 << 20),
    )(*(
        pltpu.with_memory_space_constraint(x, pltpu.HBM)
        for x in (temp, moist, mu, lit, spread, w0.T, b0[None, :], wm, bm, wf, bf[None, :])
    ))
    return pl.pallas_call(
        finish_kernel,
        out_shape=(shape, shape),
        in_specs=[vmem, vmem],
        out_specs=(hbm, hbm),
        scratch_shapes=[buf(*temp.shape), dma((2 * PARTS,))],
        compiler_params=pltpu.CompilerParams(vmem_limit_bytes=8 << 20),
    )(heat, nxt)


def on_device(
    thermal_departure,
    moisture_profile,
    solar_elevation_factor,
    daylight_groups,
    spreading_factor,
    entry_layer_matrix,
    entry_layer_offset,
    inner_layer_matrices,
    inner_layer_offsets,
    final_layer_matrix,
    final_layer_offset,
):
    return run(
        thermal_departure,
        moisture_profile,
        solar_elevation_factor,
        daylight_groups[:, 0],
        spreading_factor,
        entry_layer_matrix,
        entry_layer_offset,
        inner_layer_matrices,
        inner_layer_offsets,
        final_layer_matrix,
        final_layer_offset,
    )


def solution(mesh):
    in_specs = (
        P(None, "lat", "lon"),
        P(None, "lat", "lon"),
        P("lat", "lon"),
        P("lat", "lon"),
        P("lat", "lon"),
        P(),
        P(),
        P(),
        P(),
        P(),
        P(),
    )
    out_specs = (P(None, "lat", "lon"), P(None, "lat", "lon"))
    return jax.shard_map(
        on_device, mesh=mesh, in_specs=in_specs, out_specs=out_specs, check_vma=False
    )
```

```python
import jax
import jax.numpy as jnp
from jax import lax
from jax.experimental import pallas as pl
from jax.experimental.pallas import tpu as pltpu
from jax.sharding import PartitionSpec as P

MESH = pl.DeviceIdType.MESH
GROUP = 4
EDGE = 4
PAD = 8
REACH = 2
PREP_AT = 2
GREET_AT = 4
HALO_AT = 9
SPREAD = 5
TURNS = 8


def up(n, m):
    return (n + m - 1) // m * m


def split(x):
    hi = x.astype(jnp.bfloat16)
    lo = (x - hi.astype(jnp.float32)).astype(jnp.bfloat16)
    return hi, lo


def dot(a, b):
    return jnp.dot(a, b, preferred_element_type=jnp.float32)


def gate(h):
    return h + h * jnp.tanh(h)


def tall3(x):
    hi, lo = split(x)
    return jnp.concatenate([hi, lo, hi], axis=0)


def wide3(w):
    hi, lo = split(w)
    return jnp.concatenate([hi, hi, lo], axis=1)


def stacked(w):
    return jnp.concatenate(split(w), axis=0)


def dot3(w, x):
    hi, lo = split(x)
    n = w.shape[0] // 2
    both = dot(w, hi)
    return both[:n] + both[n:] + dot(w[:n], lo)


def roll(x, shift, axis):
    return pltpu.roll(x, shift % x.shape[axis], axis)


def kernel(
    temp, moist, mu, lit_h, spread, w0t_h, b0_h, wm_h, bm_h, wf_h, bf_h,
    heat, nxt,
    lit, w0t, b0, wm, bm, wf, bf,
    temp_v, spread_v, mu_v, mu_far, own_x, far_x,
    w0_p, w0_c, wm_c, wf_c, bm_c, bf_c,
    res_own, res_far,
    spread_t, spread_b,
    pack, left_m, left_t, left_b, right_m, right_t, right_b,
    rim, coef_0, coef_1, once,
    in_sem, own_sem, send_sem, recv_sem, put_sem, out_send, out_recv, halo_send, halo_recv,
    pair_sem,
):
    levels, rows, lanes = temp.shape
    half = rows // 2
    hid = wm_h.shape[1]
    depth = wm_h.shape[0]
    groups = half // GROUP
    feat = w0t_h.shape[0]
    kp = w0_c.shape[1]
    tiles = pack.shape[0] - 1
    slots = lanes // EDGE
    n_lat = lax.axis_size("lat")
    n_lon = lax.axis_size("lon")
    lat = lax.axis_index("lat")
    lon = lax.axis_index("lon")
    parity = lax.rem(lat, 2)
    partner = lat + 1 - 2 * parity
    mine = pl.multiple_of(parity * half, half)
    theirs = pl.multiple_of(half - parity * half, half)
    body = 2 * levels
    left = lax.rem(lon + n_lon - 1, n_lon)
    right = lax.rem(lon + 1, n_lon)
    has_up = lat > 0
    has_down = lat < n_lat - 1
    above = jnp.maximum(lat - 1, 0)
    below = jnp.minimum(lat + 1, n_lat - 1)
    leads = parity == 1
    pair_up = lat > 1
    pair_down = lat < n_lat - 2

    def at(lat_to, lon_to):
        return {"lat": lat_to, "lon": lon_to}

    def local(i, src, dst):
        return pltpu.make_async_copy(src, dst, in_sem.at[i])

    small = [
        local(0, w0t_h, w0t), local(1, lit_h, lit), local(2, b0_h, b0),
        local(3, bm_h, bm), local(4, bf_h, bf), local(5, spread, spread_v), local(6, mu, mu_v)]
    matrices = [local(7 + k, wm_h.at[k], wm.at[k]) for k in range(depth)]
    matrices.append(local(7 + depth, wf_h, wf))
    state = local(8 + depth, temp, temp_v.at[:, pl.ds(PAD, rows), :])

    def own_start(g):
        for i in range(g * GROUP, (g + 1) * GROUP):
            for src, begin in ((temp, 0), (moist, levels)):
                pltpu.make_async_copy(
                    src.at[:, mine + i, :], own_x.at[i, pl.ds(begin, levels), :],
                    own_sem.at[g]).start()

    def group_of(ref, g):
        return ref.at[pl.ds(g * GROUP, GROUP), pl.ds(0, body), :]

    def own_wait(g):
        block = group_of(own_x, g)
        pltpu.make_async_copy(block, block, own_sem.at[g]).wait()

    def swap(g, src, dst):
        return pltpu.make_async_remote_copy(
            src_ref=src, dst_ref=dst, send_sem=send_sem.at[g], recv_sem=recv_sem.at[g],
            device_id=at(partner, lon), device_id_type=MESH)

    sun_swap = swap(groups, mu.at[pl.ds(theirs, half), :], mu_far)

    def far_start(g):
        for i in range(g * GROUP, (g + 1) * GROUP):
            for src, begin in ((temp, 0), (moist, levels)):
                swap(g, src.at[:, theirs + i, :], far_x.at[i, pl.ds(begin, levels), :]).start()

    def far_wait(g):
        block = group_of(far_x, g)
        swap(g, block, block).wait()

    barrier = pltpu.get_barrier_semaphore()

    for copy in small:
        copy.start()

    @pl.when(leads)
    def _():
        pl.semaphore_signal(barrier, inc=1, device_id=at(partner, lon), device_id_type=MESH)

    own_start(0)
    own_start(1)

    @pl.when(jnp.logical_not(leads))
    def _():
        pl.semaphore_wait(barrier, 1)
        pl.semaphore_signal(pair_sem, inc=1, device_id=at(partner, lon), device_id_type=MESH)

    @pl.when(leads)
    def _():
        pl.semaphore_wait(pair_sem, 1)

        def hello(lat_to, lon_to):
            pl.semaphore_signal(
                barrier, inc=1, device_id=at(lat_to, lon_to), device_id_type=MESH)

        hello(lat, left)
        hello(lat, right)

        @pl.when(pair_up)
        def _():
            for to in (left, lon, right):
                hello(jnp.maximum(lat - 2, 0), to)

        @pl.when(pair_down)
        def _():
            for to in (left, lon, right):
                hello(jnp.minimum(lat + 2, n_lat - 1), to)

    far_start(0)
    sun_swap.start()
    far_start(1)
    for copy in matrices:
        copy.start()
    for g in range(2, groups):
        far_start(g)
        own_start(g)
    state.start()

    first, last = pl.ds(0, PAD), pl.ds(rows - PAD, PAD)

    def halo(i, src, dst, lat_to, lon_to):
        return pltpu.make_async_remote_copy(
            src_ref=src, dst_ref=dst, send_sem=halo_send.at[i], recv_sem=halo_recv.at[i],
            device_id=at(lat_to, lon_to), device_id_type=MESH)

    beside = [
        halo(0, pack, right_m, lat, left),
        halo(1, pack, left_m, lat, right),
    ]
    to_up = [
        halo(2, spread.at[first, :], spread_b, above, lon),
        halo(3, temp.at[:, pl.ds(0, REACH), :], temp_v.at[:, pl.ds(PAD + rows, REACH), :], above, lon),
        halo(4, pack.at[:, first, :], right_b, above, left),
        halo(5, pack.at[:, first, :], left_b, above, right),
    ]
    to_down = [
        halo(6, spread.at[last, :], spread_t, below, lon),
        halo(7, temp.at[:, pl.ds(rows - REACH, REACH), :],
             temp_v.at[:, pl.ds(PAD - REACH, REACH), :], below, lon),
        halo(8, pack.at[:, last, :], right_t, below, left),
        halo(9, pack.at[:, last, :], left_t, below, right),
    ]

    def clear(ref):
        ref[...] = jnp.zeros_like(ref)

    w0_p[feat:kp, :] = jnp.zeros((kp - feat, hid), jnp.float32)
    rest = own_x.shape[1] - feat
    for ref in (own_x, far_x):
        ref[:, feat:feat + rest, :] = jnp.where(
            lax.broadcasted_iota(jnp.int32, (half, rest, lanes), 1) == 0, 1.0, 0.0)

    @pl.when(jnp.logical_not(has_up))
    def _():
        temp_v[:, PAD - REACH:PAD, :] = jnp.zeros((levels, REACH, lanes), jnp.float32)
        for ref in (spread_t, left_t, right_t):
            clear(ref)

    @pl.when(jnp.logical_not(has_down))
    def _():
        temp_v[:, PAD + rows:PAD + rows + REACH, :] = jnp.zeros(
            (levels, REACH, lanes), jnp.float32)
        for ref in (spread_b, left_b, right_b):
            clear(ref)

    for copy in small:
        copy.wait()

    def column(row):
        return jnp.broadcast_to(row, (lanes, row.shape[1])).T

    w0_p[0:feat, :] = w0t[...] * 0.5
    w0_p[feat:feat + 1, :] = b0[...] * 0.5
    w0_c[...] = stacked(w0_p[...].T)
    for i in range(half):
        own_x[i, body:feat, :] = mu_v[pl.ds(mine + i, 1), :]

    def prepare(k):
        if k < depth:
            wm_c[k] = stacked(wm[k] * 0.5)
            bm_c[k] = column(bm[k:k + 1, :] * 0.5)
        else:
            wf_c[...] = wide3(wf[...])
            bf_c[...] = column(bf[...])

    def edges_of(x):
        at_lane = lax.broadcasted_iota(jnp.int32, x.shape, 1)
        acc = jnp.where(at_lane < EDGE, roll(x, 2, 1), 0.0)
        step = EDGE
        while step < lanes:
            acc = acc + roll(acc, step, 1)
            step *= 2
        return acc

    def pack_edges():
        lane = lax.broadcasted_iota(jnp.int32, (rows, lanes), 1)
        for t in range(tiles):
            count = min(slots, levels - t * slots)
            acc = jnp.zeros((rows, lanes), jnp.float32)
            for m in range(count):
                moved = roll(temp_v[t * slots + m, PAD:PAD + rows, :], EDGE * m + 2, 1)
                acc = jnp.where(lane // EDGE == m, moved, acc)
            pack[t] = acc
        pack[tiles] = edges_of(spread_v[...])

    def wide(c):
        return jnp.concatenate([c] * GROUP, axis=1)

    def load(g):
        parts, suns = [], []
        for i in range(g * GROUP, (g + 1) * GROUP):
            on = lit[mine + i].astype(jnp.float32)
            x = own_x[i] * on + far_x[i] * (1.0 - on)
            parts.append(x)
            suns.append(x[body:body + 1, :])
        x = jnp.concatenate(parts, axis=1)
        tail = jnp.zeros((kp - x.shape[0], x.shape[1]), jnp.float32)
        return jnp.concatenate([x, tail], axis=0), jnp.concatenate(suns, axis=1)

    def put(g, i):
        return pltpu.make_async_copy(
            res_own.at[i], heat.at[:, mine + i, :], put_sem.at[g])

    def send(g, i):
        return pltpu.make_async_remote_copy(
            src_ref=res_far.at[i], dst_ref=heat.at[:, mine + i, :],
            send_sem=out_send.at[g], recv_sem=out_recv.at[g],
            device_id=at(partner, lon), device_id_type=MESH)

    def finish(g, y, sun):
        y = (y + wide(bf_c[...])) * sun
        for j in range(GROUP):
            i = g * GROUP + j
            on = lit[mine + i].astype(jnp.float32)
            value = y[:, j * lanes:(j + 1) * lanes]
            res_far[i] = value * (1.0 - on)
            res_own[i] = value * on
            send(g, i).start()
            put(g, i).start()

    def greet():
        @pl.when(leads)
        def _():
            pl.semaphore_wait(
                barrier, 2 + 3 * pair_up.astype(jnp.int32) + 3 * pair_down.astype(jnp.int32))
            pl.semaphore_signal(pair_sem, inc=1, device_id=at(partner, lon), device_id_type=MESH)

        @pl.when(jnp.logical_not(leads))
        def _():
            pl.semaphore_wait(pair_sem, 1)

        for copy in beside:
            copy.start()

        @pl.when(has_up)
        def _():
            for copy in to_up:
                copy.start()

        @pl.when(has_down)
        def _():
            for copy in to_down:
                copy.start()

    tall = rows + 2 * PAD

    def stack(top, middle, bottom):
        return jnp.concatenate([top, middle, bottom], axis=0)

    def advance(x, f, west, east):
        around = roll(x, 1, 0) + roll(x, x.shape[0] - 1, 0) + west + east
        return x + f * (around - 4.0 * x)

    slot = lax.broadcasted_iota(jnp.int32, (tall, lanes), 1)
    where = lax.rem(slot, EDGE)
    zero8 = jnp.zeros((PAD, lanes), jnp.float32)

    def gather(t, here):
        lhs = stack(left_t[t], left_m[t], left_b[t])
        rhs = stack(right_t[t], right_m[t], right_b[t])
        return (jnp.where(where < 2, lhs, here), jnp.where(where < 2, here, rhs))

    def rows_ready():
        @pl.when(has_up)
        def _():
            for copy in to_down[:2]:
                copy.wait_recv()

        @pl.when(has_down)
        def _():
            for copy in to_up[:2]:
                copy.wait_recv()

        f = stack(spread_t[...], spread_v[...], spread_b[...])
        terms = (
            1.0 - 4.0 * f, f, jnp.where(slot == 0, 0.0, f), jnp.where(slot == lanes - 1, 0.0, f))
        span = coef_0.shape[1]
        for n, term in enumerate(terms):
            coef_0[n] = term[PAD - 1:PAD - 1 + span]
            coef_1[n] = term[PAD:PAD + rows]

    def sides_ready():
        for copy in beside:
            copy.wait_recv()

        @pl.when(has_up)
        def _():
            for copy in to_down[2:]:
                copy.wait_recv()

        @pl.when(has_down)
        def _():
            for copy in to_up[2:]:
                copy.wait_recv()

        f_west, f_east = gather(tiles, edges_of(stack(spread_t[...], spread_v[...], spread_b[...])))
        for t in range(tiles):
            west, east = gather(t, stack(zero8, pack[t], zero8))
            from_west, from_east = roll(west, 1, 1), roll(east, lanes - 1, 1)
            next_west = advance(west, f_west, from_west, roll(west, lanes - 1, 1))
            next_east = advance(east, f_east, roll(east, 1, 1), from_east)
            near_west = jnp.where(where == 2, f_west * from_west, 0.0)
            near_east = jnp.where(where == 1, f_east * from_east, 0.0)
            west = advance(near_west, f_west, roll(next_west, 1, 1), 0.0)
            east = advance(near_east, f_east, 0.0, roll(next_east, lanes - 1, 1))
            far_west = f_west * roll(near_west, 1, 1)
            far_east = f_east * roll(near_east, lanes - 1, 1)
            both = jnp.where(
                where < 2, jnp.where(where == 1, east, far_east),
                jnp.where(where == 2, west, far_west))
            rim[t] = both[PAD:PAD + rows]

    def spread_out(x, north, south, coef):
        return (
            x * coef[0] + (north + south) * coef[1]
            + roll(x, 1, 1) * coef[2] + roll(x, lanes - 1, 1) * coef[3])

    def diffuse(k):
        span = coef_0.shape[1]
        top = PAD - 1
        part = once.at[k % TURNS]
        part[0:span, :] = spread_out(
            temp_v[k, top:top + span, :], temp_v[k, top - 1:top - 1 + span, :],
            temp_v[k, top + 1:top + 1 + span, :], coef_0)
        nxt[k] = spread_out(
            part[1:1 + rows, :], part[0:rows, :], part[2:2 + rows, :], coef_1)

    outer = jnp.logical_or(slot[0:rows] < 2, slot[0:rows] >= lanes - 2)

    def correct(k):
        t, m = k // slots, k % slots
        turn = lanes - 2 - EDGE * m
        nxt[k] = nxt[k] + jnp.where(outer, roll(rim[t], turn, 1), 0.0)

    def some(begin, end):
        for k in range(begin, end):
            diffuse(k)

    order = [
        (g + s, layer) for g in range(0, groups, 2)
        for layer in range(depth + 2) for s in range(2)]

    def hook(event):
        if event < depth:
            prepare(event)
        if event == depth - 1:
            prepare(depth)
        if event == PREP_AT:
            state.wait()
            for g in range(2, groups):
                own_wait(g)
                far_wait(g)
            pack_edges()
        if event == GREET_AT:
            greet()
        if event == HALO_AT:
            rows_ready()
        part = event - HALO_AT
        if 0 <= part < SPREAD:
            some(levels * part // SPREAD, levels * (part + 1) // SPREAD)

    for g in range(2):
        own_wait(g)
        far_wait(g)
    sun_swap.wait()
    for copy in matrices:
        copy.wait()
    for i in range(half):
        far_x[i, body:feat, :] = mu_far[pl.ds(i, 1), :]

    suns, ready, pending = {}, {}, None

    def settle(g, layer, y):
        if layer <= depth:
            ready[g] = gate(y if layer == 0 else y + wide(bm_c[layer - 1]))
        else:
            finish(g, y, suns[g])

    for event, (g, layer) in enumerate(order):
        if layer == 0:
            ready[g], suns[g] = load(g)
        x = ready.pop(g)
        if layer == 0:
            y = dot3(w0_c[...], x)
        elif layer <= depth:
            y = dot3(wm_c[layer - 1], x)
        else:
            y = dot(wf_c[...], tall3(x))
        if pending is not None:
            settle(*pending)
        pending = (g, layer, y)
        hook(event)
    settle(*pending)
    sides_ready()
    for k in range(levels):
        correct(k)

    for copy in beside:
        copy.wait_send()

    @pl.when(has_up)
    def _():
        for copy in to_up:
            copy.wait_send()

    @pl.when(has_down)
    def _():
        for copy in to_down:
            copy.wait_send()

    for g in range(groups):
        mine_g = res_far.at[pl.ds(g * GROUP, GROUP)]
        pltpu.make_async_remote_copy(
            src_ref=mine_g, dst_ref=mine_g, send_sem=out_send.at[g], recv_sem=out_recv.at[g],
            device_id=at(partner, lon), device_id_type=MESH).wait()
        pltpu.make_async_copy(mine_g, mine_g, put_sem.at[g]).wait()


PARTS = 3


def finish_kernel(heat, nxt, out_heat, out_temp, total, sem):
    levels = heat.shape[0]
    copies = []
    cuts = [levels * p // PARTS for p in range(PARTS + 1)]
    for p in range(PARTS):
        part = pl.ds(cuts[p], cuts[p + 1] - cuts[p])
        copies.append(pltpu.make_async_copy(heat.at[part], out_heat.at[part], sem.at[p]))
        copies[-1].start()
    for p in range(PARTS):
        part = pl.ds(cuts[p], cuts[p + 1] - cuts[p])
        total[part] = nxt[part] + heat[part]
        copies.append(pltpu.make_async_copy(total.at[part], out_temp.at[part], sem.at[PARTS + p]))
        copies[-1].start()
    for copy in copies:
        copy.wait()


def run(temp, moist, mu, lit, spread, w0, b0, wm, bm, wf, bf):
    levels, rows, lanes = temp.shape
    half = rows // 2
    hid = wm.shape[1]
    depth = wm.shape[0]
    feat = w0.shape[1]
    kp = up(feat + 1, 256)
    tall = rows + 2 * PAD
    tiles = (levels * EDGE + lanes - 1) // lanes
    f32, bf16 = jnp.float32, jnp.bfloat16
    vmem = pl.BlockSpec(memory_space=pltpu.VMEM)
    hbm = pl.BlockSpec(memory_space=pltpu.HBM)
    groups = half // GROUP
    dma = pltpu.SemaphoreType.DMA

    def buf(*shape, dtype=f32):
        return pltpu.VMEM(shape, dtype)

    shape = jax.ShapeDtypeStruct(temp.shape, f32)
    heat, nxt = pl.pallas_call(
        kernel,
        out_shape=(shape, shape),
        in_specs=[hbm] * 11,
        out_specs=(vmem, vmem),
        scratch_shapes=[
            pltpu.SMEM((rows,), jnp.int32), buf(feat, hid), buf(1, hid), buf(*wm.shape),
            buf(*bm.shape), buf(*wf.shape), buf(1, levels),
            buf(levels, tall, lanes), buf(rows, lanes), buf(rows, lanes), buf(half, lanes),
            buf(half, up(feat + 1, 8), lanes), buf(half, up(feat + 1, 8), lanes),
            buf(kp, hid), buf(2 * hid, kp, dtype=bf16), buf(depth, 2 * hid, hid, dtype=bf16),
            buf(levels, 3 * hid, dtype=bf16),
            buf(depth, hid, lanes), buf(levels, lanes),
            buf(half, levels, lanes), buf(half, levels, lanes),
            buf(PAD, lanes), buf(PAD, lanes),
            buf(tiles + 1, rows, lanes),
            buf(tiles + 1, rows, lanes), buf(tiles + 1, PAD, lanes), buf(tiles + 1, PAD, lanes),
            buf(tiles + 1, rows, lanes), buf(tiles + 1, PAD, lanes), buf(tiles + 1, PAD, lanes),
            buf(tiles, rows, lanes), buf(4, rows + PAD, lanes), buf(4, rows, lanes),
            buf(TURNS, rows + PAD, lanes),
            dma((9 + depth,)), dma((groups,)), dma((groups + 1,)), dma((groups + 1,)), dma((groups,)),
            dma((groups,)), dma((groups,)), dma((10,)), dma((10,)),
            pltpu.SemaphoreType.REGULAR,
        ],
        compiler_params=pltpu.CompilerParams(
            collective_id=0, has_side_effects=True, vmem_limit_bytes=48 << 20),
    )(*(
        pltpu.with_memory_space_constraint(x, pltpu.HBM)
        for x in (temp, moist, mu, lit, spread, w0.T, b0[None, :], wm, bm, wf, bf[None, :])
    ))
    return pl.pallas_call(
        finish_kernel,
        out_shape=(shape, shape),
        in_specs=[vmem, vmem],
        out_specs=(hbm, hbm),
        scratch_shapes=[buf(*temp.shape), dma((2 * PARTS,))],
        compiler_params=pltpu.CompilerParams(vmem_limit_bytes=8 << 20),
    )(heat, nxt)


def on_device(
    thermal_departure,
    moisture_profile,
    solar_elevation_factor,
    daylight_groups,
    spreading_factor,
    entry_layer_matrix,
    entry_layer_offset,
    inner_layer_matrices,
    inner_layer_offsets,
    final_layer_matrix,
    final_layer_offset,
):
    return run(
        thermal_departure,
        moisture_profile,
        solar_elevation_factor,
        daylight_groups[:, 0],
        spreading_factor,
        entry_layer_matrix,
        entry_layer_offset,
        inner_layer_matrices,
        inner_layer_offsets,
        final_layer_matrix,
        final_layer_offset,
    )


def solution(mesh):
    in_specs = (
        P(None, "lat", "lon"),
        P(None, "lat", "lon"),
        P("lat", "lon"),
        P("lat", "lon"),
        P("lat", "lon"),
        P(),
        P(),
        P(),
        P(),
        P(),
        P(),
    )
    out_specs = (P(None, "lat", "lon"), P(None, "lat", "lon"))
    return jax.shard_map(
        on_device, mesh=mesh, in_specs=in_specs, out_specs=out_specs, check_vma=False
    )
```

```python
import jax
import jax.numpy as jnp
from jax import lax
from jax.experimental import pallas as pl
from jax.experimental.pallas import tpu as pltpu
from jax.sharding import PartitionSpec as P

MESH = pl.DeviceIdType.MESH
GROUP = 4
EDGE = 4
PAD = 8
REACH = 2
PREP_AT = 0
GREET_AT = 1
HALO_AT = 6
SPREAD = 8
TURNS = 8


def up(n, m):
    return (n + m - 1) // m * m


def split(x):
    hi = x.astype(jnp.bfloat16)
    lo = (x - hi.astype(jnp.float32)).astype(jnp.bfloat16)
    return hi, lo


def dot(a, b):
    return jnp.dot(a, b, preferred_element_type=jnp.float32)


def gate(h):
    return h + h * jnp.tanh(h)


def tall3(x):
    hi, lo = split(x)
    return jnp.concatenate([hi, lo, hi], axis=0)


def wide3(w):
    hi, lo = split(w)
    return jnp.concatenate([hi, hi, lo], axis=1)


def stacked(w):
    return jnp.concatenate(split(w), axis=0)


def dot3(w, x):
    hi, lo = split(x)
    n = w.shape[0] // 2
    both = dot(w, hi)
    return both[:n] + both[n:] + dot(w[:n], lo)


def roll(x, shift, axis):
    return pltpu.roll(x, shift % x.shape[axis], axis)


def kernel(
    temp, moist, mu, lit_h, spread, w0t_h, b0_h, wm_h, bm_h, wf_h, bf_h,
    heat, nxt,
    lit, w0t, b0, wm, bm, wf, bf,
    temp_v, spread_v, mu_v, mu_far, own_x, far_x,
    w0_p, w0_c, wm_c, wf_c, bm_c, bf_c,
    res_own, res_far,
    spread_t, spread_b,
    pack, left_m, left_t, left_b, right_m, right_t, right_b,
    rim, coef_0, coef_1, once, spread_e,
    in_sem, own_sem, send_sem, recv_sem, put_sem, out_send, out_recv, halo_send, halo_recv,
    pair_sem,
):
    levels, rows, lanes = temp.shape
    half = rows // 2
    hid = wm_h.shape[1]
    depth = wm_h.shape[0]
    groups = half // GROUP
    feat = w0t_h.shape[0]
    kp = w0_c.shape[1]
    tiles = pack.shape[0] - 1
    slots = lanes // EDGE
    n_lat = lax.axis_size("lat")
    n_lon = lax.axis_size("lon")
    lat = lax.axis_index("lat")
    lon = lax.axis_index("lon")
    parity = lax.rem(lat, 2)
    partner = lat + 1 - 2 * parity
    mine = pl.multiple_of(parity * half, half)
    theirs = pl.multiple_of(half - parity * half, half)
    body = 2 * levels
    left = lax.rem(lon + n_lon - 1, n_lon)
    right = lax.rem(lon + 1, n_lon)
    has_up = lat > 0
    has_down = lat < n_lat - 1
    above = jnp.maximum(lat - 1, 0)
    below = jnp.minimum(lat + 1, n_lat - 1)
    leads = parity == 1
    pair_up = lat > 1
    pair_down = lat < n_lat - 2

    def at(lat_to, lon_to):
        return {"lat": lat_to, "lon": lon_to}

    def local(i, src, dst):
        return pltpu.make_async_copy(src, dst, in_sem.at[i])

    small = [
        local(0, w0t_h, w0t), local(1, lit_h, lit), local(2, b0_h, b0),
        local(3, bm_h, bm), local(4, bf_h, bf), local(5, spread, spread_v), local(6, mu, mu_v)]
    matrices = [local(7 + k, wm_h.at[k], wm.at[k]) for k in range(depth)]
    matrices.append(local(7 + depth, wf_h, wf))
    state = local(8 + depth, temp, temp_v.at[:, pl.ds(PAD, rows), :])

    def own_start(g):
        for i in range(g * GROUP, (g + 1) * GROUP):
            for src, begin in ((temp, 0), (moist, levels)):
                pltpu.make_async_copy(
                    src.at[:, mine + i, :], own_x.at[i, pl.ds(begin, levels), :],
                    own_sem.at[g]).start()

    def group_of(ref, g):
        return ref.at[pl.ds(g * GROUP, GROUP), pl.ds(0, body), :]

    def own_wait(g):
        block = group_of(own_x, g)
        pltpu.make_async_copy(block, block, own_sem.at[g]).wait()

    def swap(g, src, dst):
        return pltpu.make_async_remote_copy(
            src_ref=src, dst_ref=dst, send_sem=send_sem.at[g], recv_sem=recv_sem.at[g],
            device_id=at(partner, lon), device_id_type=MESH)

    sun_swap = swap(groups, mu.at[pl.ds(theirs, half), :], mu_far)

    def far_start(g):
        for i in range(g * GROUP, (g + 1) * GROUP):
            for src, begin in ((temp, 0), (moist, levels)):
                swap(g, src.at[:, theirs + i, :], far_x.at[i, pl.ds(begin, levels), :]).start()

    def far_wait(g):
        block = group_of(far_x, g)
        swap(g, block, block).wait()

    barrier = pltpu.get_barrier_semaphore()

    for copy in small:
        copy.start()

    @pl.when(leads)
    def _():
        pl.semaphore_signal(barrier, inc=1, device_id=at(partner, lon), device_id_type=MESH)

    own_start(0)
    own_start(1)

    @pl.when(jnp.logical_not(leads))
    def _():
        pl.semaphore_wait(barrier, 1)
        pl.semaphore_signal(pair_sem, inc=1, device_id=at(partner, lon), device_id_type=MESH)

    @pl.when(leads)
    def _():
        pl.semaphore_wait(pair_sem, 1)

        def hello(lat_to, lon_to):
            pl.semaphore_signal(
                barrier, inc=1, device_id=at(lat_to, lon_to), device_id_type=MESH)

        hello(lat, left)
        hello(lat, right)

        @pl.when(pair_up)
        def _():
            for to in (left, lon, right):
                hello(jnp.maximum(lat - 2, 0), to)

        @pl.when(pair_down)
        def _():
            for to in (left, lon, right):
                hello(jnp.minimum(lat + 2, n_lat - 1), to)

    far_start(0)
    sun_swap.start()
    far_start(1)
    for copy in matrices:
        copy.start()
    for g in range(2, groups):
        far_start(g)
        own_start(g)
    state.start()

    first, last = pl.ds(0, PAD), pl.ds(rows - PAD, PAD)

    def halo(i, src, dst, lat_to, lon_to):
        return pltpu.make_async_remote_copy(
            src_ref=src, dst_ref=dst, send_sem=halo_send.at[i], recv_sem=halo_recv.at[i],
            device_id=at(lat_to, lon_to), device_id_type=MESH)

    beside = [
        halo(0, pack, right_m, lat, left),
        halo(1, pack, left_m, lat, right),
    ]
    to_up = [
        halo(2, spread.at[first, :], spread_b, above, lon),
        halo(3, temp.at[:, pl.ds(0, REACH), :], temp_v.at[:, pl.ds(PAD + rows, REACH), :], above, lon),
        halo(4, pack.at[:, first, :], right_b, above, left),
        halo(5, pack.at[:, first, :], left_b, above, right),
    ]
    to_down = [
        halo(6, spread.at[last, :], spread_t, below, lon),
        halo(7, temp.at[:, pl.ds(rows - REACH, REACH), :],
             temp_v.at[:, pl.ds(PAD - REACH, REACH), :], below, lon),
        halo(8, pack.at[:, last, :], right_t, below, left),
        halo(9, pack.at[:, last, :], left_t, below, right),
    ]

    def clear(ref):
        ref[...] = jnp.zeros_like(ref)

    w0_p[feat:kp, :] = jnp.zeros((kp - feat, hid), jnp.float32)
    rest = own_x.shape[1] - feat
    for ref in (own_x, far_x):
        ref[:, feat:feat + rest, :] = jnp.where(
            lax.broadcasted_iota(jnp.int32, (half, rest, lanes), 1) == 0, 1.0, 0.0)

    @pl.when(jnp.logical_not(has_up))
    def _():
        temp_v[:, PAD - REACH:PAD, :] = jnp.zeros((levels, REACH, lanes), jnp.float32)
        for ref in (spread_t, left_t, right_t):
            clear(ref)

    @pl.when(jnp.logical_not(has_down))
    def _():
        temp_v[:, PAD + rows:PAD + rows + REACH, :] = jnp.zeros(
            (levels, REACH, lanes), jnp.float32)
        for ref in (spread_b, left_b, right_b):
            clear(ref)

    for copy in small:
        copy.wait()

    def column(row):
        return jnp.broadcast_to(row, (lanes, row.shape[1])).T

    w0_p[0:feat, :] = w0t[...] * 0.5
    w0_p[feat:feat + 1, :] = b0[...] * 0.5
    w0_c[...] = stacked(w0_p[...].T)
    for i in range(half):
        own_x[i, body:feat, :] = mu_v[pl.ds(mine + i, 1), :]

    def prepare(k):
        if k < depth:
            wm_c[k] = stacked(wm[k] * 0.5)
            bm_c[k] = column(bm[k:k + 1, :] * 0.5)
        else:
            wf_c[...] = wide3(wf[...])
            bf_c[...] = column(bf[...])

    def edges_of(x):
        at_lane = lax.broadcasted_iota(jnp.int32, x.shape, 1)
        acc = jnp.where(at_lane < EDGE, roll(x, 2, 1), 0.0)
        step = EDGE
        while step < lanes:
            acc = acc + roll(acc, step, 1)
            step *= 2
        return acc

    def pack_edges():
        lane = lax.broadcasted_iota(jnp.int32, (rows, lanes), 1)
        for t in range(tiles):
            count = min(slots, levels - t * slots)
            acc = jnp.zeros((rows, lanes), jnp.float32)
            for m in range(count):
                moved = roll(temp_v[t * slots + m, PAD:PAD + rows, :], EDGE * m + 2, 1)
                acc = jnp.where(lane // EDGE == m, moved, acc)
            pack[t] = acc
        pack[tiles] = edges_of(spread_v[...])

    def wide(c):
        return jnp.concatenate([c] * GROUP, axis=1)

    def load(g):
        parts, suns = [], []
        for i in range(g * GROUP, (g + 1) * GROUP):
            on = lit[mine + i].astype(jnp.float32)
            x = own_x[i] * on + far_x[i] * (1.0 - on)
            parts.append(x)
            suns.append(x[body:body + 1, :])
        x = jnp.concatenate(parts, axis=1)
        tail = jnp.zeros((kp - x.shape[0], x.shape[1]), jnp.float32)
        return jnp.concatenate([x, tail], axis=0), jnp.concatenate(suns, axis=1)

    def put(g, i):
        return pltpu.make_async_copy(
            res_own.at[i], heat.at[:, mine + i, :], put_sem.at[g])

    def send(g, i):
        return pltpu.make_async_remote_copy(
            src_ref=res_far.at[i], dst_ref=heat.at[:, mine + i, :],
            send_sem=out_send.at[g], recv_sem=out_recv.at[g],
            device_id=at(partner, lon), device_id_type=MESH)

    def finish(g, y, sun):
        y = (y + wide(bf_c[...])) * sun
        for j in range(GROUP):
            i = g * GROUP + j
            on = lit[mine + i].astype(jnp.float32)
            value = y[:, j * lanes:(j + 1) * lanes]
            res_far[i] = value * (1.0 - on)
            res_own[i] = value * on
            send(g, i).start()
            put(g, i).start()

    def greet():
        @pl.when(leads)
        def _():
            pl.semaphore_wait(
                barrier, 2 + 3 * pair_up.astype(jnp.int32) + 3 * pair_down.astype(jnp.int32))
            pl.semaphore_signal(pair_sem, inc=1, device_id=at(partner, lon), device_id_type=MESH)

        @pl.when(jnp.logical_not(leads))
        def _():
            pl.semaphore_wait(pair_sem, 1)

        for copy in beside:
            copy.start()

        @pl.when(has_up)
        def _():
            for copy in to_up:
                copy.start()

        @pl.when(has_down)
        def _():
            for copy in to_down:
                copy.start()

    tall = rows + 2 * PAD

    def stack(top, middle, bottom):
        return jnp.concatenate([top, middle, bottom], axis=0)

    def advance(x, f, west, east):
        around = roll(x, 1, 0) + roll(x, x.shape[0] - 1, 0) + west + east
        return x + f * (around - 4.0 * x)

    slot = lax.broadcasted_iota(jnp.int32, (tall, lanes), 1)
    where = lax.rem(slot, EDGE)
    zero8 = jnp.zeros((PAD, lanes), jnp.float32)

    def gather(t, here):
        lhs = stack(left_t[t], left_m[t], left_b[t])
        rhs = stack(right_t[t], right_m[t], right_b[t])
        return (jnp.where(where < 2, lhs, here), jnp.where(where < 2, here, rhs))

    def rows_ready():
        @pl.when(has_up)
        def _():
            for copy in to_down[:2]:
                copy.wait_recv()

        @pl.when(has_down)
        def _():
            for copy in to_up[:2]:
                copy.wait_recv()

        f = stack(spread_t[...], spread_v[...], spread_b[...])
        terms = (
            1.0 - 4.0 * f, f, jnp.where(slot == 0, 0.0, f), jnp.where(slot == lanes - 1, 0.0, f))
        spread_e[...] = edges_of(f)
        span = coef_0.shape[1]
        for n, term in enumerate(terms):
            coef_0[n] = term[PAD - 1:PAD - 1 + span]
            coef_1[n] = term[PAD:PAD + rows]

    def sides_ready():
        for copy in beside:
            copy.wait_recv()

        @pl.when(has_up)
        def _():
            for copy in to_down[2:]:
                copy.wait_recv()

        @pl.when(has_down)
        def _():
            for copy in to_up[2:]:
                copy.wait_recv()

        f_west, f_east = gather(tiles, spread_e[...])
        for t in range(tiles):
            west, east = gather(t, stack(zero8, pack[t], zero8))
            from_west, from_east = roll(west, 1, 1), roll(east, lanes - 1, 1)
            next_west = advance(west, f_west, from_west, roll(west, lanes - 1, 1))
            next_east = advance(east, f_east, roll(east, 1, 1), from_east)
            near_west = jnp.where(where == 2, f_west * from_west, 0.0)
            near_east = jnp.where(where == 1, f_east * from_east, 0.0)
            west = advance(near_west, f_west, roll(next_west, 1, 1), 0.0)
            east = advance(near_east, f_east, 0.0, roll(next_east, lanes - 1, 1))
            far_west = f_west * roll(near_west, 1, 1)
            far_east = f_east * roll(near_east, lanes - 1, 1)
            both = jnp.where(
                where < 2, jnp.where(where == 1, east, far_east),
                jnp.where(where == 2, west, far_west))
            rim[t] = both[PAD:PAD + rows]

    def spread_out(x, north, south, coef):
        return (
            x * coef[0] + (north + south) * coef[1]
            + roll(x, 1, 1) * coef[2] + roll(x, lanes - 1, 1) * coef[3])

    def diffuse(k):
        span = coef_0.shape[1]
        top = PAD - 1
        part = once.at[k % TURNS]
        part[0:span, :] = spread_out(
            temp_v[k, top:top + span, :], temp_v[k, top - 1:top - 1 + span, :],
            temp_v[k, top + 1:top + 1 + span, :], coef_0)
        nxt[k] = spread_out(
            part[1:1 + rows, :], part[0:rows, :], part[2:2 + rows, :], coef_1)

    outer = jnp.logical_or(slot[0:rows] < 2, slot[0:rows] >= lanes - 2)

    def correct(k):
        t, m = k // slots, k % slots
        turn = lanes - 2 - EDGE * m
        nxt[k] = nxt[k] + jnp.where(outer, roll(rim[t], turn, 1), 0.0)

    def some(begin, end):
        for k in range(begin, end):
            diffuse(k)

    order = [
        (g + s, layer) for g in range(0, groups, 2)
        for layer in range(depth + 2) for s in range(2)]

    def hook(event):
        if event < depth:
            prepare(event)
        if event == depth - 1:
            prepare(depth)
        if event == PREP_AT:
            state.wait()
            for g in range(2, groups):
                own_wait(g)
                far_wait(g)
            pack_edges()
        if event == GREET_AT:
            greet()
        if event == HALO_AT:
            rows_ready()
        part = event - HALO_AT
        if 0 <= part < SPREAD:
            some(levels * part // SPREAD, levels * (part + 1) // SPREAD)

    for g in range(2):
        own_wait(g)
        far_wait(g)
    sun_swap.wait()
    for copy in matrices:
        copy.wait()
    for i in range(half):
        far_x[i, body:feat, :] = mu_far[pl.ds(i, 1), :]

    suns, ready, pending = {}, {}, None

    def settle(g, layer, y):
        if layer <= depth:
            ready[g] = gate(y if layer == 0 else y + wide(bm_c[layer - 1]))
        else:
            finish(g, y, suns[g])

    for event, (g, layer) in enumerate(order):
        if layer == 0:
            ready[g], suns[g] = load(g)
        x = ready.pop(g)
        if layer == 0:
            y = dot3(w0_c[...], x)
        elif layer <= depth:
            y = dot3(wm_c[layer - 1], x)
        else:
            y = dot(wf_c[...], tall3(x))
        if pending is not None:
            settle(*pending)
        pending = (g, layer, y)
        hook(event)
    settle(*pending)
    sides_ready()
    for k in range(levels):
        correct(k)

    for copy in beside:
        copy.wait_send()

    @pl.when(has_up)
    def _():
        for copy in to_up:
            copy.wait_send()

    @pl.when(has_down)
    def _():
        for copy in to_down:
            copy.wait_send()

    for g in range(groups):
        mine_g = res_far.at[pl.ds(g * GROUP, GROUP)]
        pltpu.make_async_remote_copy(
            src_ref=mine_g, dst_ref=mine_g, send_sem=out_send.at[g], recv_sem=out_recv.at[g],
            device_id=at(partner, lon), device_id_type=MESH).wait()
        pltpu.make_async_copy(mine_g, mine_g, put_sem.at[g]).wait()


PARTS = 3


def finish_kernel(heat, nxt, out_heat, out_temp, total, sem):
    levels = heat.shape[0]
    copies = []
    cuts = [levels * p // PARTS for p in range(PARTS + 1)]
    for p in range(PARTS):
        part = pl.ds(cuts[p], cuts[p + 1] - cuts[p])
        copies.append(pltpu.make_async_copy(heat.at[part], out_heat.at[part], sem.at[p]))
        copies[-1].start()
    for p in range(PARTS):
        part = pl.ds(cuts[p], cuts[p + 1] - cuts[p])
        total[part] = nxt[part] + heat[part]
        copies.append(pltpu.make_async_copy(total.at[part], out_temp.at[part], sem.at[PARTS + p]))
        copies[-1].start()
    for copy in copies:
        copy.wait()


def run(temp, moist, mu, lit, spread, w0, b0, wm, bm, wf, bf):
    levels, rows, lanes = temp.shape
    half = rows // 2
    hid = wm.shape[1]
    depth = wm.shape[0]
    feat = w0.shape[1]
    kp = up(feat + 1, 256)
    tall = rows + 2 * PAD
    tiles = (levels * EDGE + lanes - 1) // lanes
    f32, bf16 = jnp.float32, jnp.bfloat16
    vmem = pl.BlockSpec(memory_space=pltpu.VMEM)
    hbm = pl.BlockSpec(memory_space=pltpu.HBM)
    groups = half // GROUP
    dma = pltpu.SemaphoreType.DMA

    def buf(*shape, dtype=f32):
        return pltpu.VMEM(shape, dtype)

    shape = jax.ShapeDtypeStruct(temp.shape, f32)
    heat, nxt = pl.pallas_call(
        kernel,
        out_shape=(shape, shape),
        in_specs=[hbm] * 11,
        out_specs=(vmem, vmem),
        scratch_shapes=[
            pltpu.SMEM((rows,), jnp.int32), buf(feat, hid), buf(1, hid), buf(*wm.shape),
            buf(*bm.shape), buf(*wf.shape), buf(1, levels),
            buf(levels, tall, lanes), buf(rows, lanes), buf(rows, lanes), buf(half, lanes),
            buf(half, up(feat + 1, 8), lanes), buf(half, up(feat + 1, 8), lanes),
            buf(kp, hid), buf(2 * hid, kp, dtype=bf16), buf(depth, 2 * hid, hid, dtype=bf16),
            buf(levels, 3 * hid, dtype=bf16),
            buf(depth, hid, lanes), buf(levels, lanes),
            buf(half, levels, lanes), buf(half, levels, lanes),
            buf(PAD, lanes), buf(PAD, lanes),
            buf(tiles + 1, rows, lanes),
            buf(tiles + 1, rows, lanes), buf(tiles + 1, PAD, lanes), buf(tiles + 1, PAD, lanes),
            buf(tiles + 1, rows, lanes), buf(tiles + 1, PAD, lanes), buf(tiles + 1, PAD, lanes),
            buf(tiles, rows, lanes), buf(4, rows + PAD, lanes), buf(4, rows, lanes),
            buf(TURNS, rows + PAD, lanes), buf(tall, lanes),
            dma((9 + depth,)), dma((groups,)), dma((groups + 1,)), dma((groups + 1,)), dma((groups,)),
            dma((groups,)), dma((groups,)), dma((10,)), dma((10,)),
            pltpu.SemaphoreType.REGULAR,
        ],
        compiler_params=pltpu.CompilerParams(
            collective_id=0, has_side_effects=True, vmem_limit_bytes=48 << 20),
    )(*(
        pltpu.with_memory_space_constraint(x, pltpu.HBM)
        for x in (temp, moist, mu, lit, spread, w0.T, b0[None, :], wm, bm, wf, bf[None, :])
    ))
    return pl.pallas_call(
        finish_kernel,
        out_shape=(shape, shape),
        in_specs=[vmem, vmem],
        out_specs=(hbm, hbm),
        scratch_shapes=[buf(*temp.shape), dma((2 * PARTS,))],
        compiler_params=pltpu.CompilerParams(vmem_limit_bytes=8 << 20),
    )(heat, nxt)


def on_device(
    thermal_departure,
    moisture_profile,
    solar_elevation_factor,
    daylight_groups,
    spreading_factor,
    entry_layer_matrix,
    entry_layer_offset,
    inner_layer_matrices,
    inner_layer_offsets,
    final_layer_matrix,
    final_layer_offset,
):
    return run(
        thermal_departure,
        moisture_profile,
        solar_elevation_factor,
        daylight_groups[:, 0],
        spreading_factor,
        entry_layer_matrix,
        entry_layer_offset,
        inner_layer_matrices,
        inner_layer_offsets,
        final_layer_matrix,
        final_layer_offset,
    )


def solution(mesh):
    in_specs = (
        P(None, "lat", "lon"),
        P(None, "lat", "lon"),
        P("lat", "lon"),
        P("lat", "lon"),
        P("lat", "lon"),
        P(),
        P(),
        P(),
        P(),
        P(),
        P(),
    )
    out_specs = (P(None, "lat", "lon"), P(None, "lat", "lon"))
    return jax.shard_map(
        on_device, mesh=mesh, in_specs=in_specs, out_specs=out_specs, check_vma=False
    )
```

```python
import jax
import jax.numpy as jnp
from jax import lax
from jax.experimental import pallas as pl
from jax.experimental.pallas import tpu as pltpu
from jax.sharding import PartitionSpec as P

MESH = pl.DeviceIdType.MESH
GROUP = 4
EDGE = 4
PAD = 8
REACH = 2
PREP_AT = 0
GREET_AT = 1
HALO_AT = 6
SPREAD = 8
TURNS = 8


def up(n, m):
    return (n + m - 1) // m * m


def split(x):
    hi = x.astype(jnp.bfloat16)
    lo = (x - hi.astype(jnp.float32)).astype(jnp.bfloat16)
    return hi, lo


def dot(a, b):
    return jnp.dot(a, b, preferred_element_type=jnp.float32)


def gate(h):
    return h + h * jnp.tanh(h)


def tall3(x):
    hi, lo = split(x)
    return jnp.concatenate([hi, lo, hi], axis=0)


def wide3(w):
    hi, lo = split(w)
    return jnp.concatenate([hi, hi, lo], axis=1)


def stacked(w):
    return jnp.concatenate(split(w), axis=0)


def dot3(w, x):
    hi, lo = split(x)
    n = w.shape[0] // 2
    both = dot(w, hi)
    return both[:n] + both[n:] + dot(w[:n], lo)


def roll(x, shift, axis):
    return pltpu.roll(x, shift % x.shape[axis], axis)


def kernel(
    temp, moist, mu, lit_h, spread, w0t_h, b0_h, wm_h, bm_h, wf_h, bf_h,
    heat, nxt,
    lit, w0t, b0, wm, bm, wf, bf,
    temp_v, spread_v, mu_v, mu_far, own_x, far_x,
    w0_p, w0_c, wm_c, wf_c, bm_c, bf_c,
    res_own, res_far,
    spread_t, spread_b,
    pack, left_m, left_t, left_b, right_m, right_t, right_b,
    rim, coef_0, coef_1, once, spread_e,
    in_sem, own_sem, send_sem, recv_sem, put_sem, out_send, out_recv, halo_send, halo_recv,
    pair_sem,
):
    levels, rows, lanes = temp.shape
    half = rows // 2
    hid = wm_h.shape[1]
    depth = wm_h.shape[0]
    groups = half // GROUP
    feat = w0t_h.shape[0]
    kp = w0_c.shape[1]
    tiles = pack.shape[0] - 1
    slots = lanes // EDGE
    n_lat = lax.axis_size("lat")
    n_lon = lax.axis_size("lon")
    lat = lax.axis_index("lat")
    lon = lax.axis_index("lon")
    parity = lax.rem(lat, 2)
    partner = lat + 1 - 2 * parity
    mine = pl.multiple_of(parity * half, half)
    theirs = pl.multiple_of(half - parity * half, half)
    body = 2 * levels
    left = lax.rem(lon + n_lon - 1, n_lon)
    right = lax.rem(lon + 1, n_lon)
    has_up = lat > 0
    has_down = lat < n_lat - 1
    above = jnp.maximum(lat - 1, 0)
    below = jnp.minimum(lat + 1, n_lat - 1)
    leads = parity == 1
    pair_up = lat > 1
    pair_down = lat < n_lat - 2

    def at(lat_to, lon_to):
        return {"lat": lat_to, "lon": lon_to}

    def local(i, src, dst):
        return pltpu.make_async_copy(src, dst, in_sem.at[i])

    small = [
        local(0, w0t_h, w0t), local(1, lit_h, lit), local(2, b0_h, b0),
        local(3, bm_h, bm), local(4, bf_h, bf), local(5, spread, spread_v), local(6, mu, mu_v)]
    matrices = [local(7 + k, wm_h.at[k], wm.at[k]) for k in range(depth)]
    matrices.append(local(7 + depth, wf_h, wf))
    state = local(8 + depth, temp, temp_v.at[:, pl.ds(PAD, rows), :])

    def own_start(g):
        for i in range(g * GROUP, (g + 1) * GROUP):
            for src, begin in ((temp, 0), (moist, levels)):
                pltpu.make_async_copy(
                    src.at[:, mine + i, :], own_x.at[i, pl.ds(begin, levels), :],
                    own_sem.at[g]).start()

    def group_of(ref, g):
        return ref.at[pl.ds(g * GROUP, GROUP), pl.ds(0, body), :]

    def own_wait(g):
        block = group_of(own_x, g)
        pltpu.make_async_copy(block, block, own_sem.at[g]).wait()

    def swap(g, src, dst):
        return pltpu.make_async_remote_copy(
            src_ref=src, dst_ref=dst, send_sem=send_sem.at[g], recv_sem=recv_sem.at[g],
            device_id=at(partner, lon), device_id_type=MESH)

    sun_swap = swap(groups, mu.at[pl.ds(theirs, half), :], mu_far)

    def far_start(g):
        for i in range(g * GROUP, (g + 1) * GROUP):
            for src, begin in ((temp, 0), (moist, levels)):
                swap(g, src.at[:, theirs + i, :], far_x.at[i, pl.ds(begin, levels), :]).start()

    def far_wait(g):
        block = group_of(far_x, g)
        swap(g, block, block).wait()

    barrier = pltpu.get_barrier_semaphore()

    for copy in small:
        copy.start()

    @pl.when(leads)
    def _():
        pl.semaphore_signal(barrier, inc=1, device_id=at(partner, lon), device_id_type=MESH)

    own_start(0)
    own_start(1)

    @pl.when(jnp.logical_not(leads))
    def _():
        pl.semaphore_wait(barrier, 1)
        pl.semaphore_signal(pair_sem, inc=1, device_id=at(partner, lon), device_id_type=MESH)

    @pl.when(leads)
    def _():
        pl.semaphore_wait(pair_sem, 1)

        def hello(lat_to, lon_to):
            pl.semaphore_signal(
                barrier, inc=1, device_id=at(lat_to, lon_to), device_id_type=MESH)

        hello(lat, left)
        hello(lat, right)

        @pl.when(pair_up)
        def _():
            for to in (left, lon, right):
                hello(jnp.maximum(lat - 2, 0), to)

        @pl.when(pair_down)
        def _():
            for to in (left, lon, right):
                hello(jnp.minimum(lat + 2, n_lat - 1), to)

    far_start(0)
    sun_swap.start()
    far_start(1)
    for copy in matrices:
        copy.start()
    state.start()
    for g in range(2, groups):
        far_start(g)
        own_start(g)

    first, last = pl.ds(0, PAD), pl.ds(rows - PAD, PAD)

    def halo(i, src, dst, lat_to, lon_to):
        return pltpu.make_async_remote_copy(
            src_ref=src, dst_ref=dst, send_sem=halo_send.at[i], recv_sem=halo_recv.at[i],
            device_id=at(lat_to, lon_to), device_id_type=MESH)

    beside = [
        halo(0, pack, right_m, lat, left),
        halo(1, pack, left_m, lat, right),
    ]
    to_up = [
        halo(2, spread.at[first, :], spread_b, above, lon),
        halo(3, temp.at[:, pl.ds(0, REACH), :], temp_v.at[:, pl.ds(PAD + rows, REACH), :], above, lon),
        halo(4, pack.at[:, first, :], right_b, above, left),
        halo(5, pack.at[:, first, :], left_b, above, right),
    ]
    to_down = [
        halo(6, spread.at[last, :], spread_t, below, lon),
        halo(7, temp.at[:, pl.ds(rows - REACH, REACH), :],
             temp_v.at[:, pl.ds(PAD - REACH, REACH), :], below, lon),
        halo(8, pack.at[:, last, :], right_t, below, left),
        halo(9, pack.at[:, last, :], left_t, below, right),
    ]

    def clear(ref):
        ref[...] = jnp.zeros_like(ref)

    w0_p[feat:kp, :] = jnp.zeros((kp - feat, hid), jnp.float32)
    rest = own_x.shape[1] - feat
    for ref in (own_x, far_x):
        ref[:, feat:feat + rest, :] = jnp.where(
            lax.broadcasted_iota(jnp.int32, (half, rest, lanes), 1) == 0, 1.0, 0.0)

    @pl.when(jnp.logical_not(has_up))
    def _():
        temp_v[:, PAD - REACH:PAD, :] = jnp.zeros((levels, REACH, lanes), jnp.float32)
        for ref in (spread_t, left_t, right_t):
            clear(ref)

    @pl.when(jnp.logical_not(has_down))
    def _():
        temp_v[:, PAD + rows:PAD + rows + REACH, :] = jnp.zeros(
            (levels, REACH, lanes), jnp.float32)
        for ref in (spread_b, left_b, right_b):
            clear(ref)

    for copy in small:
        copy.wait()

    def column(row):
        return jnp.broadcast_to(row, (lanes, row.shape[1])).T

    w0_p[0:feat, :] = w0t[...] * 0.5
    w0_p[feat:feat + 1, :] = b0[...] * 0.5
    w0_c[...] = stacked(w0_p[...].T)
    for i in range(half):
        own_x[i, body:feat, :] = mu_v[pl.ds(mine + i, 1), :]

    def prepare(k):
        if k < depth:
            wm_c[k] = stacked(wm[k] * 0.5)
            bm_c[k] = column(bm[k:k + 1, :] * 0.5)
        else:
            wf_c[...] = wide3(wf[...])
            bf_c[...] = column(bf[...])

    def edges_of(x):
        at_lane = lax.broadcasted_iota(jnp.int32, x.shape, 1)
        acc = jnp.where(at_lane < EDGE, roll(x, 2, 1), 0.0)
        step = EDGE
        while step < lanes:
            acc = acc + roll(acc, step, 1)
            step *= 2
        return acc

    def pack_edges():
        lane = lax.broadcasted_iota(jnp.int32, (rows, lanes), 1)
        for t in range(tiles):
            count = min(slots, levels - t * slots)
            acc = jnp.zeros((rows, lanes), jnp.float32)
            for m in range(count):
                moved = roll(temp_v[t * slots + m, PAD:PAD + rows, :], EDGE * m + 2, 1)
                acc = jnp.where(lane // EDGE == m, moved, acc)
            pack[t] = acc
        pack[tiles] = edges_of(spread_v[...])

    def wide(c):
        return jnp.concatenate([c] * GROUP, axis=1)

    def load(g):
        parts, suns = [], []
        for i in range(g * GROUP, (g + 1) * GROUP):
            on = lit[mine + i].astype(jnp.float32)
            x = own_x[i] * on + far_x[i] * (1.0 - on)
            parts.append(x)
            suns.append(x[body:body + 1, :])
        x = jnp.concatenate(parts, axis=1)
        tail = jnp.zeros((kp - x.shape[0], x.shape[1]), jnp.float32)
        return jnp.concatenate([x, tail], axis=0), jnp.concatenate(suns, axis=1)

    def put(g, i):
        return pltpu.make_async_copy(
            res_own.at[i], heat.at[:, mine + i, :], put_sem.at[g])

    def send(g, i):
        return pltpu.make_async_remote_copy(
            src_ref=res_far.at[i], dst_ref=heat.at[:, mine + i, :],
            send_sem=out_send.at[g], recv_sem=out_recv.at[g],
            device_id=at(partner, lon), device_id_type=MESH)

    def finish(g, y, sun):
        y = (y + wide(bf_c[...])) * sun
        for j in range(GROUP):
            i = g * GROUP + j
            on = lit[mine + i].astype(jnp.float32)
            value = y[:, j * lanes:(j + 1) * lanes]
            res_far[i] = value * (1.0 - on)
            res_own[i] = value * on
            send(g, i).start()
            put(g, i).start()

    def greet():
        @pl.when(leads)
        def _():
            pl.semaphore_wait(
                barrier, 2 + 3 * pair_up.astype(jnp.int32) + 3 * pair_down.astype(jnp.int32))
            pl.semaphore_signal(pair_sem, inc=1, device_id=at(partner, lon), device_id_type=MESH)

        @pl.when(jnp.logical_not(leads))
        def _():
            pl.semaphore_wait(pair_sem, 1)

        for copy in beside:
            copy.start()

        @pl.when(has_up)
        def _():
            for copy in to_up:
                copy.start()

        @pl.when(has_down)
        def _():
            for copy in to_down:
                copy.start()

    tall = rows + 2 * PAD

    def stack(top, middle, bottom):
        return jnp.concatenate([top, middle, bottom], axis=0)

    def advance(x, f, west, east):
        around = roll(x, 1, 0) + roll(x, x.shape[0] - 1, 0) + west + east
        return x + f * (around - 4.0 * x)

    slot = lax.broadcasted_iota(jnp.int32, (tall, lanes), 1)
    where = lax.rem(slot, EDGE)
    zero8 = jnp.zeros((PAD, lanes), jnp.float32)

    def gather(t, here):
        lhs = stack(left_t[t], left_m[t], left_b[t])
        rhs = stack(right_t[t], right_m[t], right_b[t])
        return (jnp.where(where < 2, lhs, here), jnp.where(where < 2, here, rhs))

    def rows_ready():
        @pl.when(has_up)
        def _():
            for copy in to_down[:2]:
                copy.wait_recv()

        @pl.when(has_down)
        def _():
            for copy in to_up[:2]:
                copy.wait_recv()

        f = stack(spread_t[...], spread_v[...], spread_b[...])
        terms = (
            1.0 - 4.0 * f, f, jnp.where(slot == 0, 0.0, f), jnp.where(slot == lanes - 1, 0.0, f))
        spread_e[...] = edges_of(f)
        span = coef_0.shape[1]
        for n, term in enumerate(terms):
            coef_0[n] = term[PAD - 1:PAD - 1 + span]
            coef_1[n] = term[PAD:PAD + rows]

    def sides_ready():
        for copy in beside:
            copy.wait_recv()

        @pl.when(has_up)
        def _():
            for copy in to_down[2:]:
                copy.wait_recv()

        @pl.when(has_down)
        def _():
            for copy in to_up[2:]:
                copy.wait_recv()

        f_west, f_east = gather(tiles, spread_e[...])
        for t in range(tiles):
            west, east = gather(t, stack(zero8, pack[t], zero8))
            from_west, from_east = roll(west, 1, 1), roll(east, lanes - 1, 1)
            next_west = advance(west, f_west, from_west, roll(west, lanes - 1, 1))
            next_east = advance(east, f_east, roll(east, 1, 1), from_east)
            near_west = jnp.where(where == 2, f_west * from_west, 0.0)
            near_east = jnp.where(where == 1, f_east * from_east, 0.0)
            west = advance(near_west, f_west, roll(next_west, 1, 1), 0.0)
            east = advance(near_east, f_east, 0.0, roll(next_east, lanes - 1, 1))
            far_west = f_west * roll(near_west, 1, 1)
            far_east = f_east * roll(near_east, lanes - 1, 1)
            both = jnp.where(
                where < 2, jnp.where(where == 1, east, far_east),
                jnp.where(where == 2, west, far_west))
            rim[t] = both[PAD:PAD + rows]

    def spread_out(x, north, south, coef):
        return (
            x * coef[0] + (north + south) * coef[1]
            + roll(x, 1, 1) * coef[2] + roll(x, lanes - 1, 1) * coef[3])

    def diffuse(k):
        span = coef_0.shape[1]
        top = PAD - 1
        part = once.at[k % TURNS]
        part[0:span, :] = spread_out(
            temp_v[k, top:top + span, :], temp_v[k, top - 1:top - 1 + span, :],
            temp_v[k, top + 1:top + 1 + span, :], coef_0)
        nxt[k] = spread_out(
            part[1:1 + rows, :], part[0:rows, :], part[2:2 + rows, :], coef_1)

    outer = jnp.logical_or(slot[0:rows] < 2, slot[0:rows] >= lanes - 2)

    def correct(k):
        t, m = k // slots, k % slots
        turn = lanes - 2 - EDGE * m
        nxt[k] = nxt[k] + jnp.where(outer, roll(rim[t], turn, 1), 0.0)

    def some(begin, end):
        for k in range(begin, end):
            diffuse(k)

    order = [
        (g + s, layer) for g in range(0, groups, 2)
        for layer in range(depth + 2) for s in range(2)]

    def hook(event):
        if event < depth:
            prepare(event)
        if event == depth - 1:
            prepare(depth)
        if event == PREP_AT:
            state.wait()
            pack_edges()
        if event == HALO_AT:
            for g in range(2, groups):
                own_wait(g)
                far_wait(g)
        if event == GREET_AT:
            greet()
        if event == HALO_AT:
            rows_ready()
        part = event - HALO_AT
        if 0 <= part < SPREAD:
            some(levels * part // SPREAD, levels * (part + 1) // SPREAD)

    for g in range(2):
        own_wait(g)
        far_wait(g)
    sun_swap.wait()
    for copy in matrices:
        copy.wait()
    for i in range(half):
        far_x[i, body:feat, :] = mu_far[pl.ds(i, 1), :]

    suns, ready, pending = {}, {}, None

    def settle(g, layer, y):
        if layer <= depth:
            ready[g] = gate(y if layer == 0 else y + wide(bm_c[layer - 1]))
        else:
            finish(g, y, suns[g])

    for event, (g, layer) in enumerate(order):
        if layer == 0:
            ready[g], suns[g] = load(g)
        x = ready.pop(g)
        if layer == 0:
            y = dot3(w0_c[...], x)
        elif layer <= depth:
            y = dot3(wm_c[layer - 1], x)
        else:
            y = dot(wf_c[...], tall3(x))
        if pending is not None:
            settle(*pending)
        pending = (g, layer, y)
        hook(event)
    settle(*pending)
    sides_ready()
    for k in range(levels):
        correct(k)

    for copy in beside:
        copy.wait_send()

    @pl.when(has_up)
    def _():
        for copy in to_up:
            copy.wait_send()

    @pl.when(has_down)
    def _():
        for copy in to_down:
            copy.wait_send()

    for g in range(groups):
        mine_g = res_far.at[pl.ds(g * GROUP, GROUP)]
        pltpu.make_async_remote_copy(
            src_ref=mine_g, dst_ref=mine_g, send_sem=out_send.at[g], recv_sem=out_recv.at[g],
            device_id=at(partner, lon), device_id_type=MESH).wait()
        pltpu.make_async_copy(mine_g, mine_g, put_sem.at[g]).wait()


PARTS = 3


def finish_kernel(heat, nxt, out_heat, out_temp, total, sem):
    levels = heat.shape[0]
    copies = []
    cuts = [levels * p // PARTS for p in range(PARTS + 1)]
    for p in range(PARTS):
        part = pl.ds(cuts[p], cuts[p + 1] - cuts[p])
        copies.append(pltpu.make_async_copy(heat.at[part], out_heat.at[part], sem.at[p]))
        copies[-1].start()
    for p in range(PARTS):
        part = pl.ds(cuts[p], cuts[p + 1] - cuts[p])
        total[part] = nxt[part] + heat[part]
        copies.append(pltpu.make_async_copy(total.at[part], out_temp.at[part], sem.at[PARTS + p]))
        copies[-1].start()
    for copy in copies:
        copy.wait()


def run(temp, moist, mu, lit, spread, w0, b0, wm, bm, wf, bf):
    levels, rows, lanes = temp.shape
    half = rows // 2
    hid = wm.shape[1]
    depth = wm.shape[0]
    feat = w0.shape[1]
    kp = up(feat + 1, 256)
    tall = rows + 2 * PAD
    tiles = (levels * EDGE + lanes - 1) // lanes
    f32, bf16 = jnp.float32, jnp.bfloat16
    vmem = pl.BlockSpec(memory_space=pltpu.VMEM)
    hbm = pl.BlockSpec(memory_space=pltpu.HBM)
    groups = half // GROUP
    dma = pltpu.SemaphoreType.DMA

    def buf(*shape, dtype=f32):
        return pltpu.VMEM(shape, dtype)

    shape = jax.ShapeDtypeStruct(temp.shape, f32)
    heat, nxt = pl.pallas_call(
        kernel,
        out_shape=(shape, shape),
        in_specs=[hbm] * 11,
        out_specs=(vmem, vmem),
        scratch_shapes=[
            pltpu.SMEM((rows,), jnp.int32), buf(feat, hid), buf(1, hid), buf(*wm.shape),
            buf(*bm.shape), buf(*wf.shape), buf(1, levels),
            buf(levels, tall, lanes), buf(rows, lanes), buf(rows, lanes), buf(half, lanes),
            buf(half, up(feat + 1, 8), lanes), buf(half, up(feat + 1, 8), lanes),
            buf(kp, hid), buf(2 * hid, kp, dtype=bf16), buf(depth, 2 * hid, hid, dtype=bf16),
            buf(levels, 3 * hid, dtype=bf16),
            buf(depth, hid, lanes), buf(levels, lanes),
            buf(half, levels, lanes), buf(half, levels, lanes),
            buf(PAD, lanes), buf(PAD, lanes),
            buf(tiles + 1, rows, lanes),
            buf(tiles + 1, rows, lanes), buf(tiles + 1, PAD, lanes), buf(tiles + 1, PAD, lanes),
            buf(tiles + 1, rows, lanes), buf(tiles + 1, PAD, lanes), buf(tiles + 1, PAD, lanes),
            buf(tiles, rows, lanes), buf(4, rows + PAD, lanes), buf(4, rows, lanes),
            buf(TURNS, rows + PAD, lanes), buf(tall, lanes),
            dma((9 + depth,)), dma((groups,)), dma((groups + 1,)), dma((groups + 1,)), dma((groups,)),
            dma((groups,)), dma((groups,)), dma((10,)), dma((10,)),
            pltpu.SemaphoreType.REGULAR,
        ],
        compiler_params=pltpu.CompilerParams(
            collective_id=0, has_side_effects=True, vmem_limit_bytes=48 << 20),
    )(*(
        pltpu.with_memory_space_constraint(x, pltpu.HBM)
        for x in (temp, moist, mu, lit, spread, w0.T, b0[None, :], wm, bm, wf, bf[None, :])
    ))
    return pl.pallas_call(
        finish_kernel,
        out_shape=(shape, shape),
        in_specs=[vmem, vmem],
        out_specs=(hbm, hbm),
        scratch_shapes=[buf(*temp.shape), dma((2 * PARTS,))],
        compiler_params=pltpu.CompilerParams(vmem_limit_bytes=8 << 20),
    )(heat, nxt)


def on_device(
    thermal_departure,
    moisture_profile,
    solar_elevation_factor,
    daylight_groups,
    spreading_factor,
    entry_layer_matrix,
    entry_layer_offset,
    inner_layer_matrices,
    inner_layer_offsets,
    final_layer_matrix,
    final_layer_offset,
):
    return run(
        thermal_departure,
        moisture_profile,
        solar_elevation_factor,
        daylight_groups[:, 0],
        spreading_factor,
        entry_layer_matrix,
        entry_layer_offset,
        inner_layer_matrices,
        inner_layer_offsets,
        final_layer_matrix,
        final_layer_offset,
    )


def solution(mesh):
    in_specs = (
        P(None, "lat", "lon"),
        P(None, "lat", "lon"),
        P("lat", "lon"),
        P("lat", "lon"),
        P("lat", "lon"),
        P(),
        P(),
        P(),
        P(),
        P(),
        P(),
    )
    out_specs = (P(None, "lat", "lon"), P(None, "lat", "lon"))
    return jax.shard_map(
        on_device, mesh=mesh, in_specs=in_specs, out_specs=out_specs, check_vma=False
    )
```
